32 devices in a mesh: head: 4 (over z), seq: 8 (over y, x, core).
Axes of the slice: x: 2, y: 2, z: 4, core: 2. Of those that a mesh axis runs over, the one named last changes fastest.
Arguments:
- q_routed: bfloat16 [8, 8192, 128], P('head', 'seq'), may hold values from -8 to 8
- k_routed: bfloat16 [8, 8192, 128], P('head', 'seq'), may hold values from -8 to 8
- v_routed: bfloat16 [8, 8192, 128], P('head', 'seq'), may hold values from -6 to 6
- memberships: int32 [8, 8192, 1], P('head', 'seq'), may hold values from 0 to 31; in each aligned block of 1024 rows (0 to 1023, 1024 to 2047, ..., all dimensions but the last counted through in order) at most 128 rows name the same one
- q_local: bfloat16 [8, 8192, 128], P('head', 'seq'), may hold values from -8 to 8
- k_local: bfloat16 [8, 8192, 128], P('head', 'seq'), may hold values from -8 to 8
- v_local: bfloat16 [8, 8192, 128], P('head', 'seq'), may hold values from -6 to 6
Outputs:
- out_routed: bfloat16 [8, 8192, 128], P('head', 'seq')
- out_local: bfloat16 [8, 8192, 128], P('head', 'seq')
The draws below stay inside these ranges and needn't reach their ends.
Inputs may be any that keep to these rules, and one draw needn't show every extreme that they name: `memberships`: in each head, the 1024 tokens of one sequence block name any one cluster at most 128 times, a bound that some block reaches.
All inputs are finite; a program needn't handle non-finite values.
Results may differ from the reference program's by a relative error of at most 0.0049.
Values may be sent and summed in bfloat16 or wider, within the bound.
A program may use at most 64 MiB of HBM per device.

```python
import math
import jax
import jax.numpy as jnp
import numpy as np
from jax import lax

D_HEAD = 128
HALF = 8
CLUSTERS = 32
WIN = 2048
TOK_DEV = 1024
CAP = 128
SEQLEN = 8192
N_SEQ = 8


def pair_draw(key, tag):
    base = jax.random.fold_in(key, tag)
    streams = jax.random.split(base, 3)
    shape = (HALF, SEQLEN, D_HEAD)
    row_scales = jnp.exp(jax.random.uniform(streams[0], (HALF, SEQLEN, 1), jnp.float32, math.log(0.3), math.log(3.0)))
    queries = jax.random.normal(streams[1], shape, jnp.float32) * row_scales
    keys_out = jax.random.normal(streams[2], shape, jnp.float32)
    return (jnp.clip(queries, -8.0, 8.0), jnp.clip(keys_out, -8.0, 8.0))


def draw_q_routed(key, part):
    return pair_draw(key, 11)[0].astype(jnp.bfloat16)


def draw_k_routed(key, part):
    return pair_draw(key, 11)[1].astype(jnp.bfloat16)


def draw_q_local(key, part):
    return pair_draw(key, 23)[0].astype(jnp.bfloat16)


def draw_k_local(key, part):
    return pair_draw(key, 23)[1].astype(jnp.bfloat16)


def block_scale(own_key, dims, cuts, least, largest):
    factor_of = 1.0
    for axis_at, parts in cuts:
        heights = jax.random.uniform(jax.random.fold_in(jax.random.fold_in(own_key, 6), axis_at), (parts,), jnp.float32, least / len(cuts), largest / len(cuts))
        factor_of = factor_of * jnp.repeat(jnp.exp(heights), dims[axis_at] // parts).reshape((-1,) + (1,) * (len(dims) - 1 - axis_at))
    return factor_of


def shared_out(stream_key, own, number, rows, count, top, limit, skew):
    order = jax.random.permutation(stream_key, count)
    heavy_load, ordinary = portions_of(count, rows * top, limit, skew, True), portions_of(count, rows * top, limit, skew, False)
    places = jnp.arange(count)

    def named(lengths, turn):
        used = int((lengths > 0).sum())
        fixed = max(1, used // 4)
        shifted = fixed + (places - fixed + turn * (used - fixed)) % max(1, count - fixed)
        return jnp.zeros((count,), jnp.int32).at[order[jnp.where(places < fixed, places, shifted)]].set(jnp.asarray(lengths, jnp.int32))

    lengths = jnp.where(number % 4 == 0, named(heavy_load, number // 4), named(ordinary, number - number // 4 - 1))
    mixed = jax.random.permutation(jax.random.fold_in(own, 3), count)
    donor, sink = mixed[0:count // 2 * 2:2], mixed[1:count // 2 * 2:2]
    slack = jnp.minimum(lengths[donor] - 1, limit - lengths[sink]) // 2
    slack = jnp.where((donor == order[0]) | (sink == order[0]) | (lengths[sink] == 0), 0, jnp.maximum(slack, 0))
    shifted = jax.random.randint(jax.random.fold_in(own, 4), (count // 2,), 0, 1 << 20) % (slack + 1)
    lengths = lengths.at[donor].add(-shifted).at[sink].add(shifted)
    items = jnp.searchsorted(jnp.cumsum(lengths), jnp.arange(rows * top), side="right").astype(jnp.int32)
    grid = items.reshape(top, rows).T
    grid = grid[jax.random.permutation(jax.random.fold_in(own, 1), rows)]
    turn = jax.random.randint(jax.random.fold_in(own, 2), (rows, 1), 0, top)
    return jnp.take_along_axis(grid, (jnp.arange(top)[None, :] + turn) % top, axis=1)


def portions_of(number_of, total, reach, slope, full):
    loads = [(1 << 20) // math.isqrt(rank ** slope) + 1 for rank in range(1, number_of + 1)]
    largest = reach if full else min(reach, max(-(-total // number_of), total * loads[0] // sum(loads)))
    least = 1 if total - largest >= number_of - 1 else 0
    counts, rest = [largest] + [least] * (number_of - 1), total - largest - least * (number_of - 1)
    while rest > 0:
        movable = [i for i in range(1, number_of) if counts[i] < largest] or [i for i in range(1, number_of) if counts[i] < reach]
        pool, budget = sum([loads[i] for i in movable]), rest
        for i in movable:
            extra = min(reach - counts[i], max(1, budget * loads[i] // pool), rest)
            counts[i] = counts[i] + extra
            rest = rest - extra
    return np.array(counts)


def scatter_about(stream_key, extent, deviation, reach, pieces=(), kind=jnp.bfloat16):
    array = jax.random.normal(stream_key, extent, jnp.float32) * deviation
    if len(pieces) > 0:
        array = block_scale(stream_key, extent, pieces, -0.22, 0.18) * array
    return jnp.clip(array, min=-reach, max=reach).astype(kind)


def setup_inputs(seed: int = 0) -> dict:
    keys = jax.random.split(jax.random.key(seed), 8)
    q_routed = draw_q_routed(jax.random.fold_in(keys[7], 71), 0)
    k_routed = draw_k_routed(jax.random.fold_in(keys[7], 71), 0)
    v_routed = scatter_about(keys[2], (HALF, SEQLEN, D_HEAD), 1.0, 6.0, ((0, 4), (1, 8)))
    memberships_keys = jax.random.split(jax.random.fold_in(keys[3], 1), HALF * SEQLEN // TOK_DEV)
    memberships_turns = jax.random.permutation(jax.random.fold_in(keys[3], 3), HALF * SEQLEN // TOK_DEV)
    memberships = jax.vmap(lambda own, number: shared_out(jax.random.fold_in(keys[3], 2), own, number, TOK_DEV, CLUSTERS, 1, CAP, 2))(memberships_keys, memberships_turns).reshape((HALF, SEQLEN, 1))
    q_local = draw_q_local(jax.random.fold_in(keys[7], 71), 0)
    k_local = draw_k_local(jax.random.fold_in(keys[7], 71), 0)
    v_local = scatter_about(keys[6], (HALF, SEQLEN, D_HEAD), 1.0, 6.0, ((0, 4), (1, 8)))
    return {"q_routed": q_routed, "k_routed": k_routed, "v_routed": v_routed, "memberships": memberships, "q_local": q_local, "k_local": k_local, "v_local": v_local}


def mix_rows(scores, allowed, value_rows):
    scores = jnp.where(allowed, scores, -1e30)
    row_max = jnp.max(scores, axis=-1, keepdims=True)
    exponent = jnp.exp(scores - row_max)
    row_total = jnp.sum(exponent, axis=-1, keepdims=True)
    weights = (exponent / row_total).astype(jnp.bfloat16)
    mixed = jnp.dot(weights.astype(jnp.float32), value_rows.astype(jnp.float32), preferred_element_type=jnp.float32)
    return mixed.astype(jnp.bfloat16)


def block_scores(query_block, key_block):
    score_scale = D_HEAD ** -0.5
    return jnp.dot(query_block.astype(jnp.float32), key_block.astype(jnp.float32).T, preferred_element_type=jnp.float32) * score_scale


def routed_head(inputs):
    queries, keys_in, values_in, cluster_ids = inputs
    positions = jnp.arange(SEQLEN, dtype=jnp.int32)
    order = jnp.argsort(cluster_ids * SEQLEN + positions).astype(jnp.int32)
    sorted_q = queries[order]
    sorted_ids = cluster_ids[order]
    sorted_pos = positions[order]
    reach_rows = N_SEQ * CAP
    pad_keys = jnp.concatenate([jnp.zeros((reach_rows, D_HEAD), keys_in.dtype), keys_in[order]], axis=0)
    pad_values = jnp.concatenate([jnp.zeros((reach_rows, D_HEAD), values_in.dtype), values_in[order]], axis=0)
    pad_ids = jnp.concatenate([jnp.full((reach_rows,), -1, jnp.int32), sorted_ids], axis=0)
    pad_pos = jnp.concatenate([jnp.zeros((reach_rows,), jnp.int32), sorted_pos], axis=0)
    block_rows = min(512, SEQLEN)

    def one_block(block_index):
        first_row = (block_index * block_rows).astype(jnp.int32)
        query_block = lax.dynamic_slice_in_dim(sorted_q, first_row, block_rows, 0)
        query_ids = lax.dynamic_slice_in_dim(sorted_ids, first_row, block_rows, 0)
        query_pos = lax.dynamic_slice_in_dim(sorted_pos, first_row, block_rows, 0)
        key_block = lax.dynamic_slice_in_dim(pad_keys, first_row, reach_rows + block_rows, 0)
        value_block = lax.dynamic_slice_in_dim(pad_values, first_row, reach_rows + block_rows, 0)
        id_block = lax.dynamic_slice_in_dim(pad_ids, first_row, reach_rows + block_rows, 0)
        pos_block = lax.dynamic_slice_in_dim(pad_pos, first_row, reach_rows + block_rows, 0)
        allowed = (id_block[None, :] == query_ids[:, None]) & (pos_block[None, :] <= query_pos[:, None])
        return mix_rows(block_scores(query_block, key_block), allowed, value_block)

    mixed = lax.map(one_block, jnp.arange(SEQLEN // block_rows, dtype=jnp.int32)).reshape(SEQLEN, D_HEAD)
    return jnp.zeros_like(mixed).at[order].set(mixed)


def local_head(inputs):
    queries, keys_in, values_in = inputs
    pad_keys = jnp.concatenate([jnp.zeros((WIN, D_HEAD), keys_in.dtype), keys_in], axis=0)
    pad_values = jnp.concatenate([jnp.zeros((WIN, D_HEAD), values_in.dtype), values_in], axis=0)
    block_rows = min(512, SEQLEN)

    def one_block(block_index):
        first_row = (block_index * block_rows).astype(jnp.int32)
        query_block = lax.dynamic_slice_in_dim(queries, first_row, block_rows, 0)
        key_block = lax.dynamic_slice_in_dim(pad_keys, first_row, WIN + block_rows, 0)
        value_block = lax.dynamic_slice_in_dim(pad_values, first_row, WIN + block_rows, 0)
        query_pos = first_row + jnp.arange(block_rows, dtype=jnp.int32)
        key_pos = first_row - WIN + jnp.arange(WIN + block_rows, dtype=jnp.int32)
        distance_back = query_pos[:, None] - key_pos[None, :]
        allowed = (key_pos[None, :] >= 0) & (distance_back >= 0) & (distance_back < WIN)
        return mix_rows(block_scores(query_block, key_block), allowed, value_block)

    return lax.map(one_block, jnp.arange(SEQLEN // block_rows, dtype=jnp.int32)).reshape(SEQLEN, D_HEAD)


def reference(q_routed, k_routed, v_routed, memberships, q_local, k_local, v_local):
    out_routed = lax.map(routed_head, (q_routed, k_routed, v_routed, memberships[:, :, 0]))
    out_local = lax.map(local_head, (q_local, k_local, v_local))
    return (out_routed, out_local)
```

```python
import functools

import jax
import jax.numpy as jnp
from jax import lax
from jax.experimental import pallas as pl
from jax.experimental.pallas import tpu as pltpu
from jax.sharding import PartitionSpec as P

WIN = 2048
PENALTY = 32768.0
NEG = -1e30
LOG2E = 1.4426950408889634
ID_ROWS = 16


def dot_t(a, b):
    return lax.dot_general(a, b, (((1,), (1,)), ((), ())), preferred_element_type=jnp.float32)


def one_hot_rows(id_rows, tok):
    classes = lax.broadcasted_iota(jnp.int32, (128, 128), 0).astype(jnp.float32)
    parts = []
    for row in range(tok // 128):
        hot = jnp.where(id_rows[row : row + 1, :] == classes, 1.0, 0.0)
        parts.append(hot.T)
    return jnp.concatenate(parts, axis=0)


def routed_kernel(
    count, first, last, tok, tile, scale, flags, q_ref, own_ref, *refs
):
    kv_refs = refs[:count]
    refs = refs[count:]
    if not first:
        m_in, acc_in = refs[:2]
        refs = refs[2:]
    if last:
        out_ref = refs[0]
        refs = refs[1:]
    else:
        m_out, acc_out = refs[:2]
        refs = refs[2:]
    m_s, acc_s, qext, kext, vext = refs
    factor = scale * LOG2E

    if first:
        m_s[...] = jnp.full(m_s.shape, NEG, jnp.float32)
        acc_s[...] = jnp.zeros(acc_s.shape, jnp.float32)
    else:
        m_s[...] = m_in[0]
        acc_s[...] = acc_in[0]
    vext[:, 128:] = jnp.ones((tok, 128), jnp.bfloat16)
    qext[:, :128] = q_ref[0]
    own_ids = own_ref[0].astype(jnp.float32)
    qext[:, 128:] = ((one_hot_rows(own_ids, tok) - 1.0) * PENALTY).astype(jnp.bfloat16)

    for index in range(count):
        diagonal = first and index == 0

        @pl.when(flags[index] > 0)
        def _():
            ref = kv_refs[index]
            kext[:, :128] = ref[0, :tok]
            vext[:, :128] = ref[0, tok : 2 * tok]
            ids = ref[0, 2 * tok : 2 * tok + ID_ROWS].astype(jnp.float32)
            kext[:, 128:] = one_hot_rows(ids, tok).astype(jnp.bfloat16)
            for start in range(0, tok, tile):
                rows = pl.ds(start, tile)
                width = start + tile if diagonal else tok
                s = dot_t(qext[rows, :], kext[:width, :])
                if diagonal:
                    row = lax.broadcasted_iota(jnp.int32, (tile, tile), 0)
                    col = lax.broadcasted_iota(jnp.int32, (tile, tile), 1)
                    tail = jnp.where(col <= row, s[:, start:], NEG)
                    s = tail if start == 0 else jnp.concatenate([s[:, :start], tail], axis=1)
                m_old = m_s[rows, :]
                m_new = jnp.maximum(m_old, jnp.max(s, axis=1, keepdims=True))
                alpha = jnp.exp2((m_old - m_new) * factor)
                p = jnp.exp2((s - m_new[:, :1]) * factor).astype(jnp.bfloat16)
                add = jnp.dot(p, vext[:width, :], preferred_element_type=jnp.float32)
                acc = acc_s[rows, :]
                acc_s[rows, :] = acc * jnp.concatenate([alpha, alpha], axis=1) + add
                m_s[rows, :] = m_new

    if last:
        out_ref[0] = (acc_s[:, :128] / acc_s[:, 128:]).astype(jnp.bfloat16)
    else:
        m_out[0] = m_s[...]
        acc_out[0] = acc_s[...]


def routed_step(q, packed_own, chunks, flags, state, last):
    heads, tok, width = q.shape
    count = len(chunks)
    rows = packed_own.shape[1]
    first = state is None
    tile = min(256, tok)

    def whole(shape):
        return pl.BlockSpec((1,) + shape, lambda h, f: (h, 0, 0))

    id_block = 2 * tok // ID_ROWS
    in_specs = [whole((tok, width)), pl.BlockSpec((1, ID_ROWS, width), lambda h, f: (h, id_block, 0))]
    in_specs += [whole((rows, width))] * count
    args = [q, packed_own] + list(chunks)
    if not first:
        in_specs += [whole((tok, 128)), whole((tok, 256))]
        args += list(state)
    if last:
        out_shape = jax.ShapeDtypeStruct((heads, tok, width), jnp.bfloat16)
        out_specs = whole((tok, width))
    else:
        out_shape = (
            jax.ShapeDtypeStruct((heads, tok, 128), jnp.float32),
            jax.ShapeDtypeStruct((heads, tok, 256), jnp.float32),
        )
        out_specs = (whole((tok, 128)), whole((tok, 256)))
    return pl.pallas_call(
        functools.partial(routed_kernel, count, first, last, tok, tile, width ** (-0.5)),
        out_shape=out_shape,
        grid_spec=pltpu.PrefetchScalarGridSpec(
            num_scalar_prefetch=1,
            grid=(heads,),
            in_specs=in_specs,
            out_specs=out_specs,
            scratch_shapes=[
                pltpu.VMEM((tok, 128), jnp.float32),
                pltpu.VMEM((tok, 256), jnp.float32),
                pltpu.VMEM((tok, 256), jnp.bfloat16),
                pltpu.VMEM((tok, 256), jnp.bfloat16),
                pltpu.VMEM((tok, 256), jnp.bfloat16),
            ],
        ),
        cost_estimate=pl.CostEstimate(
            flops=heads * count * tok * tok * 1024,
            bytes_accessed=heads * count * rows * width * 2,
            transcendentals=heads * count * tok * tok,
        ),
        name=f"routed_{count}_{int(first)}{int(last)}",
    )(flags, *args)


def local_kernel(reach, tok, tile, scale, flags, q_ref, *refs):
    kv_refs = refs[: reach + 1]
    out_ref, qext, kext, vext = refs[reach + 1 :]
    factor = scale * LOG2E
    lane = lax.broadcasted_iota(jnp.int32, (tok, 128), 1)
    qext[:, :128] = q_ref[0]
    qext[:, 128:] = jnp.where(lane == 0, -PENALTY, 0.0).astype(jnp.bfloat16)
    vext[:, 128:] = jnp.ones(((reach + 1) * tok, 128), jnp.bfloat16)
    for index in range(reach + 1):
        rows = pl.ds(index * tok, tok)
        kext[rows, :128] = kv_refs[index][0, :tok]
        vext[rows, :128] = kv_refs[index][0, tok : 2 * tok]
        absent = jnp.where(flags[index] > 0, 0.0, 1.0)
        kext[rows, 128:] = jnp.full((tok, 128), absent, jnp.float32).astype(jnp.bfloat16)
    row = lax.broadcasted_iota(jnp.int32, (tile, tile), 0)
    col = lax.broadcasted_iota(jnp.int32, (tile, tile), 1)
    span = reach * tok + tile
    for start in range(0, tok, tile):
        rows = pl.ds(start, tile)
        keys = pl.ds(start, span)
        s = dot_t(qext[rows, :], kext[keys, :])
        head = jnp.where(col > row, s[:, :tile], NEG)
        tail = jnp.where(col <= row, s[:, span - tile :], NEG)
        s = jnp.concatenate([head, s[:, tile : span - tile], tail], axis=1)
        top = jnp.max(s, axis=1, keepdims=True)
        p = jnp.exp2((s - top) * factor).astype(jnp.bfloat16)
        acc = jnp.dot(p, vext[keys, :], preferred_element_type=jnp.float32)
        out_ref[0, rows, :] = (acc[:, :128] / acc[:, 128:]).astype(jnp.bfloat16)


def local_step(q, blocks, flags):
    heads, tok, width = q.shape
    reach = len(blocks) - 1
    tile = min(256, tok)

    def whole(shape):
        return pl.BlockSpec((1,) + shape, lambda h, f: (h, 0, 0))

    return pl.pallas_call(
        functools.partial(local_kernel, reach, tok, tile, width ** (-0.5)),
        out_shape=jax.ShapeDtypeStruct((heads, tok, width), jnp.bfloat16),
        grid_spec=pltpu.PrefetchScalarGridSpec(
            num_scalar_prefetch=1,
            grid=(heads,),
            in_specs=[whole((tok, width))] + [whole((2 * tok, width))] * (reach + 1),
            out_specs=whole((tok, width)),
            scratch_shapes=[
                pltpu.VMEM((tok, 256), jnp.bfloat16),
                pltpu.VMEM(((reach + 1) * tok, 256), jnp.bfloat16),
                pltpu.VMEM(((reach + 1) * tok, 256), jnp.bfloat16),
            ],
        ),
        cost_estimate=pl.CostEstimate(
            flops=heads * (reach * tok + tile) * tok * 1024,
            bytes_accessed=heads * (reach + 2) * tok * width * 4,
            transcendentals=heads * (reach * tok + tile) * tok,
        ),
        name="windowed",
    )(flags, q, *blocks)


def move(value, pairs):
    return lax.ppermute(value, "seq", pairs)


def local(q_routed, k_routed, v_routed, memberships, q_local, k_local, v_local):
    count = lax.axis_size("seq")
    me = lax.axis_index("seq")
    heads, tok, width = q_routed.shape
    id_rows = memberships.reshape(heads, tok // 128, 128).astype(jnp.bfloat16)
    id_rows = jnp.pad(id_rows, ((0, 0), (0, ID_ROWS - tok // 128), (0, 0)))
    packed = jnp.concatenate([k_routed, v_routed, id_rows], axis=1)
    windowed = jnp.concatenate([k_local, v_local], axis=1)
    reach = WIN // tok
    swap = [(i, i ^ 1) for i in range(count)]
    odd = me % 2 == 1

    def ordered(sources):
        return jnp.stack([(source < me).astype(jnp.int32) for source in sources])

    def earlier_blocks(after):
        mine, _ = lax.optimization_barrier((windowed, after))
        if reach == 2 and count % 2 == 0:
            far = move(mine, [(i, i + 2) for i in range(count - 2)])
            near = move(jnp.where(odd, far, windowed), swap)
            return [far, near]
        return [move(mine, [(i, i + d) for i in range(count - d)]) for d in range(reach, 0, -1)]

    if count == 8:
        from_x = move(packed, [(i, i ^ 2) for i in (0, 1, 4, 5)])
        from_y = move(packed, [(i, i ^ 4) for i in (0, 1, 2, 3)])
        partner = move(packed, [(i, i ^ 1) for i in (0, 2, 4, 6)])
        chip = me // 2
        relay = jnp.where(chip == 1, from_x, from_y)
        from_far = move(relay, [(2, 6), (3, 7), (6, 4), (7, 5)])
        far_source = jnp.where(chip == 3, me ^ 6, jnp.where(chip == 2, me ^ 6, count))
        x_other = move(from_x, swap)
        y_other = move(from_y, swap)
        far_other = move(from_far, swap)
        blocks = earlier_blocks(from_x)
        state = routed_step(
            q_routed, packed, [packed, partner],
            jnp.stack([jnp.int32(1), odd.astype(jnp.int32)]), None, False,
        )
        state = routed_step(
            q_routed, packed, [from_x, x_other], ordered([me ^ 2, me ^ 3]), state, False
        )
        state = routed_step(
            q_routed, packed, [from_y, y_other], ordered([me ^ 4, me ^ 5]), state, False
        )
        out_routed = routed_step(
            q_routed, packed, [from_far, far_other], ordered([far_source, far_source]), state, True
        )
    else:
        blocks = earlier_blocks(packed)
        gathered = lax.all_gather(packed, "seq")
        group = 4
        state = routed_step(
            q_routed, packed, [packed], jnp.ones((1,), jnp.int32), None, count == 1
        )
        for start in range(0, count, group):
            sources = range(start, min(count, start + group))
            state = routed_step(
                q_routed, packed, [gathered[i] for i in sources], ordered(sources), state,
                start + group >= count,
            )
        out_routed = state
    present = [(me >= d).astype(jnp.int32) for d in range(reach, -1, -1)]
    out_local = local_step(q_local, blocks + [windowed], jnp.stack(present))
    return (out_routed, out_local)


def solution(mesh):
    placed = (P("head", "seq", None),) * 7
    return jax.shard_map(
        local,
        mesh=mesh,
        in_specs=placed,
        out_specs=(P("head", "seq", None), P("head", "seq", None)),
        check_vma=False,
    )
```
